32 devices in a mesh: row: 8 (over z, core), col: 4 (over y, x).
Axes of the slice: x: 2, y: 2, z: 4, core: 2. Of those that a mesh axis runs over, the one named last changes fastest.
Arguments:
- example_grads: bfloat16 [1024, 4096], P(('row', 'col')), may hold values from -6 to 6
- val_grads: bfloat16 [64, 4096], P('row'), may hold values from -6 to 6
- val_weight: float32 [64], replicated, may hold values from 0.25 to 4
Outputs:
- gram: bfloat16 [1024, 640], P('row', 'col')
- weighted: float32 [1024, 64], P(('row', 'col'))
- scores: float32 [1024], P(('row', 'col'))
The draws below stay inside these ranges and needn't reach their ends.
All inputs are finite; a program needn't handle non-finite values.
Results may differ from the reference program's by a relative error of at most 0.0034.
Values may be sent and summed in bfloat16 or wider, within the bound.
No kernel may reach another device: no remote copies, remote signals or barrier semaphores. Data moves between devices by JAX's collectives and lax.ppermute only.
A program may use at most 64 MiB of HBM per device.

```python
import math
import jax
import jax.numpy as jnp
from jax import lax

D = 4096
ROWS_DEV = 32
N = 1024
M = 64
N_ROW = 8
N_COL = 4


def block_scale(key, shape, shards, smallest, high):
    def one(axis_at, shards_of):
        draws = jax.random.uniform(jax.random.fold_in(jax.random.fold_in(key, 6), axis_at), (shards_of,), jnp.float32, smallest / len(shards), high / len(shards))
        return jnp.repeat(jnp.exp(draws), shape[axis_at] // shards_of).reshape((-1,) + (1,) * (len(shape) - axis_at - 1))

    gain = one(*shards[0])
    for cut in shards[1:]:
        gain = gain * one(*cut)
    return gain


def bell_draw(key, dims, spread, most, cuts=(), held_as=jnp.bfloat16):
    drawn = jax.random.normal(key, dims, jnp.float32) * spread
    if len(cuts) > 0:
        drawn = block_scale(key, dims, cuts, -0.22, 0.18) * drawn
    return jnp.clip(drawn, min=-most, max=most).astype(held_as)


def setup_inputs(seed: int = 0) -> dict:
    streams_of = jax.random.split(jax.random.key(seed), 4)
    example_grads = bell_draw(streams_of[0], (N, D), 1.0, 6.0, ((0, 32),))
    val_grads = bell_draw(streams_of[1], (M, D), 1.0, 6.0, ((0, 8),))
    val_weight = jnp.clip(jnp.exp(jax.random.uniform(streams_of[2], (M,), jnp.float32, math.log(0.25), math.log(4.0))), 0.25, 4.0)
    return dict(example_grads=example_grads, val_grads=val_grads, val_weight=val_weight)


step_size = 0.5


def reference(example_grads, val_grads, val_weight):
    total = example_grads.shape[0]
    feature_width = example_grads.shape[1]
    val_count = val_grads.shape[0]
    half = N_ROW // 2
    slots = half + 1
    block_rows = ROWS_DEV * N_COL
    exact = example_grads.astype(jnp.float32)
    val_products = (jnp.dot(exact, val_grads.astype(jnp.float32).T, precision=lax.Precision.HIGHEST) * (feature_width ** -0.5)).astype(jnp.bfloat16)
    product_values = val_products.astype(jnp.float32)
    grid_grads = exact.reshape(N_ROW, N_COL, ROWS_DEV, feature_width)
    grid_values = product_values.reshape(N_ROW, N_COL, ROWS_DEV, val_count)
    slot_of = (jnp.arange(N_COL * slots * ROWS_DEV, dtype=jnp.int32) // ROWS_DEV) % slots

    def one_block(carry, block_index):
        start = block_index * block_rows
        rows = lax.dynamic_slice_in_dim(exact, start, block_rows, 0)
        row_values = lax.dynamic_slice_in_dim(product_values, start, block_rows, 0)
        rolled = jnp.roll(grid_grads, -block_index, axis=0)[:slots].transpose(1, 0, 2, 3).reshape(-1, feature_width)
        rolled_values = jnp.roll(grid_values, -block_index, axis=0)[:slots].transpose(1, 0, 2, 3).reshape(-1, val_count)
        dropped = jnp.logical_and(slot_of == half, block_index >= half)
        tile = (jnp.dot(rows, rolled.T, precision=lax.Precision.HIGHEST) * (1.0 / feature_width)).astype(jnp.bfloat16)
        tile = jnp.where(dropped[None, :], jnp.zeros_like(tile), tile)
        tile_values = tile.astype(jnp.float32)
        direct = jnp.dot(tile_values, rolled_values, precision=lax.Precision.HIGHEST)
        mirrored = jnp.dot(tile_values.T, row_values, precision=lax.Precision.HIGHEST)
        mirrored = jnp.where((slot_of == 0)[:, None], jnp.zeros_like(mirrored), mirrored)
        mirrored = mirrored.reshape(N_COL, slots, ROWS_DEV, val_count).transpose(1, 0, 2, 3)
        placed = jnp.zeros((N_ROW, N_COL, ROWS_DEV, val_count), jnp.float32).at[:slots].set(mirrored)
        placed = jnp.roll(placed, block_index, axis=0)
        return carry + placed.reshape(total, val_count), (tile, direct)

    start_carry = jnp.zeros((total, val_count), jnp.float32)
    carried, outputs = lax.scan(one_block, start_carry, jnp.arange(N_ROW, dtype=jnp.int32))
    tiles, direct = outputs
    gram = tiles.reshape(total, N_COL * slots * ROWS_DEV)
    weighted = direct.reshape(total, val_count) + carried
    scores = jnp.dot(product_values - step_size * weighted, val_weight, precision=lax.Precision.HIGHEST) * (val_count ** -0.5)
    return gram, weighted, scores
```

```python
import jax
import jax.numpy as jnp
from jax import lax
from jax.experimental import pallas as pl
from jax.experimental.pallas import tpu as pltpu
from jax.sharding import PartitionSpec as P


step_size = 0.5


CONTRACT_LAST = (((1,), (1,)), ((), ()))
CONTRACT_FIRST = (((0,), (0,)), ((), ()))


def product(a, b, contract=CONTRACT_LAST):
    return lax.dot_general(a, b, contract, preferred_element_type=jnp.float32)


def place(col, k, count):
    return pl.ds(pl.multiple_of(jnp.bitwise_xor(col, k) * count, count), count)


def early_kernel(rows_total, cols_total, refs):
    half, quarter = rows_total // 2, rows_total // 4
    xy, same, other, vals_in = refs["xy"], refs["same"], refs["other"], refs["vals"]
    left, vals, row_val_ref = refs["left"], refs["all_vals"], refs["row_val"]
    right = refs["right"]
    count, width = xy[0].shape
    val_rows = vals_in[0].shape[0]
    row = lax.axis_index("row")
    col = lax.axis_index("col")
    low = lax.rem(row, 2) == 0
    for k in range(cols_total):
        left[place(col, k, count), :] = xy[k][...]
    for t in range(quarter):
        right[2 * t * count : (2 * t + 1) * count, :] = same[t][...]
    for t in range(quarter - 1):
        at = slice((2 * t + 1) * count, (2 * t + 2) * count)

        @pl.when(low)
        def _():
            right[at, :] = other[t][...]

        @pl.when(jnp.logical_not(low))
        def _():
            right[at, :] = other[t + 1][...]

    swapped = vals_in[half]
    for t in range(half):
        at = pl.multiple_of(lax.rem(row + 2 * t, rows_total) * val_rows, val_rows)
        vals[pl.ds(at, val_rows), :] = vals_in[t][...]
        near = jnp.bitwise_xor(row, 1)
        at = pl.multiple_of(lax.rem(near + 2 * t, rows_total) * val_rows, val_rows)
        vals[pl.ds(at, val_rows), :] = swapped[t * val_rows : (t + 1) * val_rows, :]
    root = width ** (-0.5)
    tile = (product(right[...], left[...]) * (1.0 / width)).astype(jnp.bfloat16)
    row_val = (product(left[...], vals[...]) * root).astype(jnp.bfloat16)
    col_val = (product(right[...], vals[...]) * root).astype(jnp.bfloat16)
    refs["tile"][...] = tile
    row_val_ref[...] = row_val
    refs["own_val"][...] = col_val[:count].astype(jnp.float32)
    refs["sums"][...] = product(tile, col_val, CONTRACT_FIRST)
    mirrored = jnp.dot(tile, row_val, preferred_element_type=jnp.float32)
    for j, ref in enumerate(refs["mirrored"], 1):
        ref[...] = mirrored[j * count : (j + 1) * count]


def late_kernel(rows_total, refs):
    half = rows_total // 2
    left, vals, row_val, right = refs["left"], refs["all_vals"], refs["row_val"], refs["right"]
    count, width = refs["same"].shape
    row = lax.axis_index("row")
    col = lax.axis_index("col")
    low = lax.rem(row, 2) == 0

    @pl.when(low)
    def _():
        right[:count, :] = refs["other_near"][...]

    @pl.when(jnp.logical_not(low))
    def _():
        right[:count, :] = refs["other_far"][...]

    right[count:, :] = refs["same"][...]
    tile = product(right[...], left[...]) * (1.0 / width)
    last = lax.broadcasted_iota(jnp.int32, tile.shape, 0) >= count
    dropped = jnp.logical_and(last, row >= half)
    tile = jnp.where(dropped, 0.0, tile).astype(jnp.bfloat16)
    col_val = (product(right[...], vals[...]) * width ** (-0.5)).astype(jnp.bfloat16)
    done = refs["tile"].shape[0]
    refs["gram"][:done, :] = refs["tile"][...]
    refs["gram"][done:, :] = tile
    refs["total"][...] = refs["sums"][...] + product(tile, col_val, CONTRACT_FIRST)
    mirrored = jnp.dot(tile, row_val[...], preferred_element_type=jnp.float32)
    for k, ref in enumerate(refs["direct"]):
        ref[...] = refs["total"][place(col, k, count), :]
    for j, ref in enumerate(refs["mirrored"]):
        ref[...] = mirrored[j * count : (j + 1) * count]


def call(body, ins, outs, scratch):
    groups = [(key, value) for part in (ins, outs, scratch) for key, value in part.items()]
    flat = lambda part: [v for value in part.values() for v in (value if isinstance(value, list) else [value])]

    def kernel(*refs):
        refs, named = list(refs), {}
        for key, value in groups:
            if isinstance(value, list):
                named[key], refs = refs[: len(value)], refs[len(value) :]
            else:
                named[key], refs = refs[0], refs[1:]
        body(named)

    vmem = pl.BlockSpec(memory_space=pltpu.VMEM)
    got = pl.pallas_call(
        kernel,
        out_shape=flat(outs),
        in_specs=[vmem] * len(flat(ins)),
        out_specs=[vmem] * len(flat(outs)),
        scratch_shapes=[pltpu.VMEM(s.shape, s.dtype) for s in flat(scratch)],
        compiler_params=pltpu.CompilerParams(vmem_limit_bytes=32 * 1024 * 1024),
    )(*flat(ins))
    got, named = list(got), {}
    for key, value in outs.items():
        if isinstance(value, list):
            named[key], got = got[: len(value)], got[len(value) :]
        else:
            named[key], got = got[0], got[1:]
    return named


def on_device(example_grads, val_grads, val_weight):
    count, width = example_grads.shape
    val_count = val_weight.shape[0]
    rows_total = lax.axis_size("row")
    cols_total = lax.axis_size("col")
    half, quarter = rows_total // 2, rows_total // 4
    slots, block = half + 1, cols_total * count
    assert rows_total % 4 == 0 and cols_total & (cols_total - 1) == 0

    def xor_col(value, k):
        return lax.ppermute(value, "col", [(i, i ^ k) for i in range(cols_total)])

    def from_row(value, j):
        return lax.ppermute(value, "row", [((i + j) % rows_total, i) for i in range(rows_total)])

    def swap(value):
        return lax.ppermute(value, "row", [(i ^ 1, i) for i in range(rows_total)])

    def to_row(value, j):
        senders = rows_total if j < half else half
        return lax.ppermute(value, "row", [(i, (i + j) % rows_total) for i in range(senders)])

    same = [example_grads]
    for _ in range(1, quarter):
        same.append(from_row(same[-1], 2))
    pairs = [((i + 2) % rows_total, i) for i in range(rows_total) if i % 2 == 0 or i < half]
    same.append(lax.ppermute(same[-1], "row", pairs))
    other = [swap(same[t]) for t in range(quarter + 1)]
    xy = [example_grads] + [xor_col(example_grads, k) for k in range(1, cols_total)]
    vals = [val_grads] + [from_row(val_grads, 2 * t) for t in range(1, half)]
    joined = jnp.concatenate(vals, axis=0)
    vals.append(swap(joined))

    f32 = lambda *shape: jax.ShapeDtypeStruct(shape, jnp.float32)
    bf16 = lambda *shape: jax.ShapeDtypeStruct(shape, jnp.bfloat16)
    early = call(
        lambda refs: early_kernel(rows_total, cols_total, refs),
        dict(xy=xy, same=same[:quarter], other=other[:quarter], vals=vals),
        dict(
            tile=bf16((slots - 2) * count, block),
            left=bf16(block, width),
            all_vals=bf16(val_count, width),
            row_val=bf16(block, val_count),
            own_val=f32(count, val_count),
            sums=f32(block, val_count),
            mirrored=[f32(count, val_count)] * (slots - 3),
        ),
        dict(right=bf16((slots - 2) * count, width)),
    )
    carried = {key: early[key] for key in ("tile", "left", "all_vals", "row_val", "sums")}
    late = call(
        lambda refs: late_kernel(rows_total, refs),
        dict(carried, same=same[quarter], other_near=other[quarter - 1], other_far=other[quarter]),
        dict(
            gram=bf16(slots * count, block),
            direct=[f32(count, val_count)] * cols_total,
            mirrored=[f32(count, val_count)] * 2,
        ),
        dict(right=bf16(2 * count, width), total=f32(block, val_count)),
    )
    mirrored = early["mirrored"] + late["mirrored"]
    weighted = late["direct"][0]
    for k in range(1, cols_total):
        weighted = weighted + xor_col(late["direct"][k], k)
    for j, value in enumerate(mirrored, 1):
        weighted = weighted + to_row(value, j)
    scaled = val_weight * val_count ** (-0.5)
    scores = jnp.sum((early["own_val"] - step_size * weighted) * scaled[None, :], axis=1)
    return late["gram"].T, weighted, scores


def solution(mesh):
    in_specs = (P(("row", "col"), None), P("row", None), P())
    out_specs = (P("row", "col"), P(("row", "col"), None), P(("row", "col")))

    return jax.shard_map(
        on_device, mesh=mesh, in_specs=in_specs, out_specs=out_specs, check_vma=False
    )
```
